32 devices in a mesh: row: 2 (over x), col: 8 (over z, core), freq: 2 (over y).
Axes of the slice: x: 2, y: 2, z: 4, core: 2. Of those that a mesh axis runs over, the one named last changes fastest.
Arguments:
- left_data: float32 [2, 2048, 512], P(None, ('freq', 'row'), 'col'), parts along dimension 1, may hold values from -6 to 6
- right_data: float32 [2, 512, 8192], P(None, 'row', ('freq', 'col')), parts along dimension 2, may hold values from -0.1875 to 0.1875
Outputs:
- multiples: float32 [2, 2048, 4096], P(None, ('freq', 'row'), 'col'), parts along dimension 1
The draws below stay inside these ranges and needn't reach their ends.
There are 2 independent parts, one for each index of `freq`. The reference program is written for one: setup_inputs(seed, part) draws one part's arguments, and reference() takes and returns one part's arrays. A program takes and returns all parts, laid end to end along the dimension named above; each array names one. Nothing has to cross between parts.
All inputs are finite; a program needn't handle non-finite values.
Results may differ from the reference program's by a relative error of at most 0.000071.
Values sent between devices are 32-bit elements; how exact they have to be, the bound alone decides.
A program may use at most 64 MiB of HBM per device.

```python
import jax
import jax.numpy as jnp
from jax import lax

KW = 512
MR = 1024
MC = 4096


def level_of(own_key, extent, pieces, least, high):
    gain, own = 1.0, jax.random.fold_in(own_key, 6)
    for dim, shards_of in pieces:
        steps = jnp.exp(jax.random.uniform(jax.random.fold_in(own, dim), (shards_of,), jnp.float32, least / len(pieces), high / len(pieces)))
        gain = gain * jnp.repeat(steps, extent[dim] // shards_of).reshape([-1 if axis == dim else 1 for axis in range(len(extent))])
    return gain


def scatter_about(own_key, shape, deviation, most, pieces=(), dtype=jnp.bfloat16):
    drawn = deviation * jax.random.normal(own_key, shape, jnp.float32)
    if pieces:
        drawn = drawn * level_of(own_key, shape, pieces, -0.22, 0.18)
    return jnp.clip(drawn, -most, most).astype(dtype)


def setup_inputs(seed: int = 0, part: int = 0) -> dict:
    key_list = jax.random.split(jax.random.key(seed), 3)
    own_keys = jax.random.split(jax.random.fold_in(key_list[2], part), 3)
    left_data = scatter_about(own_keys[0], (2, MR, KW), 1.0, 6.0, ((1, 2), (2, 8)), jnp.float32)
    right_data = scatter_about(own_keys[1], (2, KW, MC), (2 * KW) ** -0.5, 0.1875, ((1, 2), (2, 8)), jnp.float32)
    return dict(left_data=left_data, right_data=right_data)


def matmul_hi(a, b):
    return jnp.dot(a, b, preferred_element_type=jnp.float32, precision=lax.Precision.HIGHEST)


def reference(left_data, right_data):
    real_part = matmul_hi(left_data[0], right_data[0]) - matmul_hi(left_data[1], right_data[1])
    imag_part = matmul_hi(left_data[0], right_data[1]) + matmul_hi(left_data[1], right_data[0])
    return jnp.stack([real_part, imag_part], axis=0)
```

```python
import functools

import jax
import jax.numpy as jnp
from jax import lax
from jax.experimental import pallas as pl
from jax.experimental.pallas import tpu as pltpu
from jax.sharding import PartitionSpec as P

MESH = pl.DeviceIdType.MESH
LANES = 128


def split(value):
    high = value.astype(jnp.bfloat16)
    return high, (value - high.astype(jnp.float32)).astype(jnp.bfloat16)


def dot(a, b):
    return jnp.dot(a, b, preferred_element_type=jnp.float32)


def kernel(
    n_row, n_col, left_hbm, right_hbm, out_ref,
    left_f32, right_f32, left_hi, left_lo, w_hi, w_lo,
    own_sem, left_send, left_recv, right_send, right_recv,
):
    _, kb, rows = left_hbm.shape
    _, kr, cols = right_hbm.shape
    depth = kb * n_col
    chunks = cols // LANES
    line = n_col // 2

    x = lax.axis_index("row")
    place = lax.axis_index("col")
    z, core = place // 2, lax.rem(place, 2)
    has_next, has_prev = z + 1 < line, z >= 1

    def at(zz, cc):
        return {"col": zz * 2 + cc}

    def peer(d):
        return lax.rem(x + d, n_row)

    barrier = pltpu.get_barrier_semaphore()
    for d in range(1, n_row):
        pl.semaphore_signal(barrier, inc=1, device_id={"row": peer(d)}, device_id_type=MESH)

    @pl.when(has_next)
    def _():
        pl.semaphore_signal(barrier, inc=1, device_id=at(z + 1, core), device_id_type=MESH)

    @pl.when(has_prev)
    def _():
        pl.semaphore_signal(barrier, inc=1, device_id=at(z - 1, core), device_id_type=MESH)

    pl.semaphore_signal(barrier, inc=1, device_id=at(z, 1 - core), device_id_type=MESH)

    own_right = pltpu.make_async_copy(
        right_hbm, right_f32.at[:, pl.ds(pl.multiple_of(x * kr, 8), kr), :], own_sem.at[0])
    own_right.start()
    own_left = pltpu.make_async_copy(
        left_hbm, left_f32.at[:, pl.ds(pl.multiple_of(place * kb, 8), kb), :], own_sem.at[1])
    own_left.start()

    pl.semaphore_wait(barrier, n_row + has_next.astype(jnp.int32) + has_prev.astype(jnp.int32))

    def right_copy(d, j):
        return pltpu.make_async_remote_copy(
            src_ref=right_hbm.at[:, :, pl.ds(j * LANES, LANES)],
            dst_ref=right_f32.at[:, pl.ds(pl.multiple_of(x * kr, 8), kr), pl.ds(j * LANES, LANES)],
            send_sem=right_send.at[d - 1, j],
            recv_sem=right_recv.at[d - 1, j],
            device_id={"row": peer(d)},
            device_id_type=MESH,
        )

    def left_slot(zz, cc, part):
        return left_f32.at[part, pl.ds(pl.multiple_of((zz * 2 + cc) * kb, 8), kb), :]

    def left_copy(way, zz, cc, part, target, own=False):
        return pltpu.make_async_remote_copy(
            src_ref=left_hbm.at[part] if own else left_slot(zz, cc, part),
            dst_ref=left_slot(zz, cc, part),
            send_sem=left_send.at[way, zz, part],
            recv_sem=left_recv.at[cc, zz, part],
            device_id=target,
            device_id_type=MESH,
        )

    def up(zz, part, own=False):
        return left_copy(0, zz, core, part, at(z + 1, core), own)

    def down(zz, part, own=False):
        return left_copy(1, zz, core, part, at(z - 1, core), own)

    def across(zz, part, own=False):
        return left_copy(2, zz, core, part, at(z, 1 - core), own)

    def arrived(zz, cc, part):
        left_copy(2, zz, cc, part, at(z, 1 - core)).wait_recv()

    for part in range(2):
        @pl.when(has_next)
        def _():
            up(z, part, True).start()

        @pl.when(has_prev)
        def _():
            down(z, part, True).start()

    for j in range(chunks):
        for d in range(1, n_row):
            right_copy(d, j).start()
    for part in range(2):
        across(z, part, True).start()

    def to_weights(source_row, j, n):
        span = pl.ds(pl.multiple_of(source_row, 8), n)
        re = split(right_f32[0, span, j * LANES:(j + 1) * LANES])
        im = split(right_f32[1, span, j * LANES:(j + 1) * LANES])
        below = pl.ds(pl.multiple_of(depth + source_row, 8), n)
        for w, a, b in ((w_hi, re[0], im[0]), (w_lo, re[1], im[1])):
            w[j, span, :LANES] = a
            w[j, span, LANES:] = b
            w[j, below, :LANES] = -b
            w[j, below, LANES:] = a

    def convert(g):
        for part in range(2):
            block = left_f32[part, pl.ds(pl.multiple_of(g * LANES, LANES), LANES), :].T
            high, low = split(block)
            where = pl.ds(pl.multiple_of(part * depth + g * LANES, LANES), LANES)
            left_hi[:, where] = high
            left_lo[:, where] = low

    def partner_arrived(zz):
        for part in range(2):
            arrived(zz, 1 - core, part)

    def settle(zz):
        partner_arrived(zz)
        if 2 * kb == LANES:
            convert(zz)

    def right_arrived(j):
        for d in range(1, n_row):
            right_copy(d, j).wait_recv()
            to_weights(lax.rem(x + n_row - d, n_row) * kr, j, kr)

    own_right.wait()
    for j in range(chunks):
        to_weights(x * kr, j, kr)
    own_left.wait()

    for d in range(1, line):
        for part in range(2):
            @pl.when(z - d >= 0)
            def _():
                arrived(z - d, core, part)

                @pl.when(has_next)
                def _():
                    up(z - d, part).start()

                across(z - d, part).start()

            @pl.when(z + d < line)
            def _():
                arrived(z + d, core, part)

                @pl.when(has_prev)
                def _():
                    down(z + d, part).start()

                across(z + d, part).start()

        if d == 1:
            settle(z)
        else:
            @pl.when(z - (d - 1) >= 0)
            def _():
                settle(z - (d - 1))

            @pl.when(z + (d - 1) < line)
            def _():
                settle(z + (d - 1))

        if d - 1 < chunks - 1:
            right_arrived(d - 1)

    if line == 1:
        settle(z)
    else:
        @pl.when(z - (line - 1) >= 0)
        def _():
            settle(z - (line - 1))

        @pl.when(z + (line - 1) < line)
        def _():
            settle(z + (line - 1))

    if 2 * kb != LANES:
        for g in range(depth // LANES):
            convert(g)

    for j in range(chunks):
        if j >= min(line - 1, chunks - 1):
            right_arrived(j)
        total = dot(left_hi[...], w_hi[j]) + (dot(left_hi[...], w_lo[j]) + dot(left_lo[...], w_hi[j]))
        out_ref[0, :, j * LANES:(j + 1) * LANES] = total[:, :LANES]
        out_ref[1, :, j * LANES:(j + 1) * LANES] = total[:, LANES:]

    for j in range(chunks):
        for d in range(1, n_row):
            right_copy(d, j).wait_send()
    for part in range(2):
        for d in range(line):
            own = d == 0

            @pl.when(z - d >= 0)
            def _():
                @pl.when(has_next)
                def _():
                    up(z - d, part, own).wait_send()

                across(z - d, part, own).wait_send()

            @pl.when(z + d < line)
            def _():
                @pl.when(has_prev)
                def _():
                    down(z + d, part, own).wait_send()

                if d > 0:
                    across(z + d, part).wait_send()


def body(n_row, n_col, left_data, right_data):
    left = jnp.swapaxes(left_data, 1, 2)
    _, kb, rows = left.shape
    _, kr, cols = right_data.shape
    depth, chunks, line = kb * n_col, cols // LANES, n_col // 2
    return pl.pallas_call(
        functools.partial(kernel, n_row, n_col),
        out_shape=jax.ShapeDtypeStruct((2, rows, cols), jnp.float32),
        in_specs=[pl.BlockSpec(memory_space=pl.ANY)] * 2,
        out_specs=pl.BlockSpec(memory_space=pltpu.VMEM),
        scratch_shapes=[
            pltpu.VMEM((2, depth, rows), jnp.float32),
            pltpu.VMEM((2, depth, cols), jnp.float32),
            pltpu.VMEM((rows, 2 * depth), jnp.bfloat16),
            pltpu.VMEM((rows, 2 * depth), jnp.bfloat16),
            pltpu.VMEM((chunks, 2 * depth, 2 * LANES), jnp.bfloat16),
            pltpu.VMEM((chunks, 2 * depth, 2 * LANES), jnp.bfloat16),
            pltpu.SemaphoreType.DMA((2,)),
            pltpu.SemaphoreType.DMA((3, line, 2)),
            pltpu.SemaphoreType.DMA((2, line, 2)),
            pltpu.SemaphoreType.DMA((n_row - 1, chunks)),
            pltpu.SemaphoreType.DMA((n_row - 1, chunks)),
        ],
        compiler_params=pltpu.CompilerParams(
            collective_id=0, has_side_effects=True, vmem_limit_bytes=48 * 1024 * 1024),
    )(left, right_data)


def solution(mesh):
    placed = (P(None, ("freq", "row"), "col"), P(None, "row", ("freq", "col")))
    return jax.shard_map(
        functools.partial(body, mesh.shape["row"], mesh.shape["col"]),
        mesh=mesh, in_specs=placed, out_specs=P(None, ("freq", "row"), "col"), check_vma=False,
    )
```

```python
import functools

import jax
import jax.numpy as jnp
from jax import lax
from jax.experimental import pallas as pl
from jax.experimental.pallas import tpu as pltpu
from jax.sharding import PartitionSpec as P

MESH = pl.DeviceIdType.MESH
LANES = 128


def split(value):
    high = value.astype(jnp.bfloat16)
    return high, (value - high.astype(jnp.float32)).astype(jnp.bfloat16)


def dot(a, b):
    return jnp.dot(a, b, preferred_element_type=jnp.float32)


def three_dots(left_hi, left_lo, w_hi, w_lo):
    return dot(left_hi, w_hi) + (dot(left_hi, w_lo) + dot(left_lo, w_hi))


def in_turn(kr):
    return kr % LANES == 0


def finish(first, done_ref, own_part, left_hi, left_lo, w_hi, w_lo, out_hbm, tail, sem):
    rows, ready = done_ref.shape[1:]
    early = pltpu.make_async_copy(done_ref, out_hbm.at[:, :, pl.ds(0, ready)], sem.at[0])
    early.start()
    copies = [early]
    half = rows // 2
    j = w_hi.shape[0] - 1
    for i in range(2):
        span = pl.ds(i * half, half)
        total = own_part[span, :] + three_dots(
            left_hi[span, first:], left_lo[span, first:], w_hi[j, first:, :], w_lo[j, first:, :])
        tail[0, span, :] = total[:, :LANES]
        tail[1, span, :] = total[:, LANES:]
        copy = pltpu.make_async_copy(
            tail.at[:, span, :], out_hbm.at[:, span, pl.ds(ready, LANES)], sem.at[1 + i])
        copy.start()
        copies.append(copy)
    for copy in copies:
        copy.wait()


def kernel(
    n_row, n_col, left_hbm, right_hbm, out_ref, own_part, left_hi, left_lo, w_hi, w_lo,
    left_f32, right_f32, own_sem, left_send, left_recv, right_send, right_recv,
):
    _, kb, rows = left_hbm.shape
    _, kr, cols = right_hbm.shape
    depth = kb * n_col
    chunks = cols // LANES
    line = n_col // 2

    x = lax.axis_index("row")
    place = lax.axis_index("col")
    z, core = place // 2, lax.rem(place, 2)
    has_next, has_prev = z + 1 < line, z >= 1

    def at(zz, cc):
        return {"col": zz * 2 + cc}

    def peer(d):
        return lax.rem(x + d, n_row)

    barrier = pltpu.get_barrier_semaphore()
    for d in range(1, n_row):
        pl.semaphore_signal(barrier, inc=1, device_id={"row": peer(d)}, device_id_type=MESH)

    @pl.when(has_next)
    def _():
        pl.semaphore_signal(barrier, inc=1, device_id=at(z + 1, core), device_id_type=MESH)

    @pl.when(has_prev)
    def _():
        pl.semaphore_signal(barrier, inc=1, device_id=at(z - 1, core), device_id_type=MESH)

    pl.semaphore_signal(barrier, inc=1, device_id=at(z, 1 - core), device_id_type=MESH)

    own_right = pltpu.make_async_copy(
        right_hbm, right_f32.at[:, pl.ds(pl.multiple_of(x * kr, 8), kr), :], own_sem.at[0])
    own_right.start()
    own_left = pltpu.make_async_copy(
        left_hbm, left_f32.at[:, pl.ds(pl.multiple_of(place * kb, 8), kb), :], own_sem.at[1])
    own_left.start()

    pl.semaphore_wait(barrier, n_row + has_next.astype(jnp.int32) + has_prev.astype(jnp.int32))

    def right_copy(d, j):
        return pltpu.make_async_remote_copy(
            src_ref=right_hbm.at[:, :, pl.ds(j * LANES, LANES)],
            dst_ref=right_f32.at[:, pl.ds(pl.multiple_of(x * kr, 8), kr), pl.ds(j * LANES, LANES)],
            send_sem=right_send.at[d - 1, j],
            recv_sem=right_recv.at[d - 1, j],
            device_id={"row": peer(d)},
            device_id_type=MESH,
        )

    def left_slot(zz, cc, part):
        return left_f32.at[part, pl.ds(pl.multiple_of((zz * 2 + cc) * kb, 8), kb), :]

    def left_copy(way, zz, cc, part, target, own=False):
        return pltpu.make_async_remote_copy(
            src_ref=left_hbm.at[part] if own else left_slot(zz, cc, part),
            dst_ref=left_slot(zz, cc, part),
            send_sem=left_send.at[way, zz, part],
            recv_sem=left_recv.at[cc, zz, part],
            device_id=target,
            device_id_type=MESH,
        )

    def up(zz, part, own=False):
        return left_copy(0, zz, core, part, at(z + 1, core), own)

    def down(zz, part, own=False):
        return left_copy(1, zz, core, part, at(z - 1, core), own)

    def across(zz, part, own=False):
        return left_copy(2, zz, core, part, at(z, 1 - core), own)

    def arrived(zz, cc, part):
        left_copy(2, zz, cc, part, at(z, 1 - core)).wait_recv()

    for part in range(2):
        @pl.when(has_next)
        def _():
            up(z, part, True).start()

        @pl.when(has_prev)
        def _():
            down(z, part, True).start()

    for j in range(chunks):
        for d in range(1, n_row):
            right_copy(d, j).start()
    for part in range(2):
        across(z, part, True).start()

    def to_weights(d, j):
        owner = peer(d)
        span = pl.ds(pl.multiple_of(owner * kr, 8), kr)
        re = split(right_f32[0, span, j * LANES:(j + 1) * LANES])
        im = split(right_f32[1, span, j * LANES:(j + 1) * LANES])
        if in_turn(kr):
            above, below = pl.ds(2 * d * kr, kr), pl.ds((2 * d + 1) * kr, kr)
        else:
            above, below = span, pl.ds(pl.multiple_of(depth + owner * kr, 8), kr)
        for w, a, b in ((w_hi, re[0], im[0]), (w_lo, re[1], im[1])):
            w[j, above, :LANES] = a
            w[j, above, LANES:] = b
            w[j, below, :LANES] = -b
            w[j, below, LANES:] = a

    def convert(g):
        for part in range(2):
            block = left_f32[part, pl.ds(pl.multiple_of(g * LANES, LANES), LANES), :].T
            high, low = split(block)
            if in_turn(kr):
                owner = g * LANES // kr
                turn = lax.rem(owner - x + n_row, n_row)
                first = (2 * turn + part) * kr + g * LANES - owner * kr
            else:
                first = part * depth + g * LANES
            where = pl.ds(pl.multiple_of(first, LANES), LANES)
            left_hi[:, where] = high
            left_lo[:, where] = low

    def early_part():
        if in_turn(kr):
            n = 2 * kr
            own_part[...] = three_dots(
                left_hi[:, :n], left_lo[:, :n], w_hi[chunks - 1, :n, :], w_lo[chunks - 1, :n, :])
        else:
            own_part[...] = jnp.zeros_like(own_part)

    def partner_arrived(zz):
        for part in range(2):
            arrived(zz, 1 - core, part)

    def settle(zz):
        partner_arrived(zz)
        if 2 * kb == LANES:
            convert(zz)

    def right_arrived(j):
        for d in range(1, n_row):
            right_copy(d, j).wait_recv()
            to_weights(n_row - d, j)

    own_right.wait()
    for j in range(chunks):
        to_weights(0, j)
    own_left.wait()

    for d in range(1, line):
        for part in range(2):
            @pl.when(z - d >= 0)
            def _():
                arrived(z - d, core, part)

                @pl.when(has_next)
                def _():
                    up(z - d, part).start()

                across(z - d, part).start()

            @pl.when(z + d < line)
            def _():
                arrived(z + d, core, part)

                @pl.when(has_prev)
                def _():
                    down(z + d, part).start()

                across(z + d, part).start()

        if d == 1:
            settle(z)
        else:
            @pl.when(z - (d - 1) >= 0)
            def _():
                settle(z - (d - 1))

            @pl.when(z + (d - 1) < line)
            def _():
                settle(z + (d - 1))

        if d - 1 < chunks - 1:
            right_arrived(d - 1)

    if line == 1:
        settle(z)
    else:
        @pl.when(z - (line - 1) >= 0)
        def _():
            settle(z - (line - 1))

        @pl.when(z + (line - 1) < line)
        def _():
            settle(z + (line - 1))

    if 2 * kb != LANES:
        for g in range(depth // LANES):
            convert(g)

    for j in range(chunks - 1):
        if j >= line - 1:
            right_arrived(j)
        total = three_dots(left_hi[...], left_lo[...], w_hi[j], w_lo[j])
        out_ref[0, :, j * LANES:(j + 1) * LANES] = total[:, :LANES]
        out_ref[1, :, j * LANES:(j + 1) * LANES] = total[:, LANES:]
        if j == chunks - 3 or (j == 0 and chunks < 3):
            early_part()
    right_arrived(chunks - 1)

    for j in range(chunks):
        for d in range(1, n_row):
            right_copy(d, j).wait_send()
    for part in range(2):
        for d in range(line):
            own = d == 0

            @pl.when(z - d >= 0)
            def _():
                @pl.when(has_next)
                def _():
                    up(z - d, part, own).wait_send()

                across(z - d, part, own).wait_send()

            @pl.when(z + d < line)
            def _():
                @pl.when(has_prev)
                def _():
                    down(z + d, part, own).wait_send()

                if d > 0:
                    across(z + d, part).wait_send()


def body(n_row, n_col, left_data, right_data):
    left = jnp.swapaxes(left_data, 1, 2)
    _, kb, rows = left.shape
    _, kr, cols = right_data.shape
    depth, chunks, line = kb * n_col, cols // LANES, n_col // 2
    vmem = pl.BlockSpec(memory_space=pltpu.VMEM)
    held = pl.pallas_call(
        functools.partial(kernel, n_row, n_col),
        out_shape=[
            jax.ShapeDtypeStruct((2, rows, cols - LANES), jnp.float32),
            jax.ShapeDtypeStruct((rows, 2 * LANES), jnp.float32),
            jax.ShapeDtypeStruct((rows, 2 * depth), jnp.bfloat16),
            jax.ShapeDtypeStruct((rows, 2 * depth), jnp.bfloat16),
            jax.ShapeDtypeStruct((chunks, 2 * depth, 2 * LANES), jnp.bfloat16),
            jax.ShapeDtypeStruct((chunks, 2 * depth, 2 * LANES), jnp.bfloat16),
        ],
        in_specs=[pl.BlockSpec(memory_space=pltpu.HBM)] * 2,
        out_specs=[vmem] * 6,
        scratch_shapes=[
            pltpu.VMEM((2, depth, rows), jnp.float32),
            pltpu.VMEM((2, depth, cols), jnp.float32),
            pltpu.SemaphoreType.DMA((2,)),
            pltpu.SemaphoreType.DMA((3, line, 2)),
            pltpu.SemaphoreType.DMA((2, line, 2)),
            pltpu.SemaphoreType.DMA((n_row - 1, chunks)),
            pltpu.SemaphoreType.DMA((n_row - 1, chunks)),
        ],
        compiler_params=pltpu.CompilerParams(
            collective_id=0, has_side_effects=True, vmem_limit_bytes=32 * 1024 * 1024),
    )(left, right_data)
    return pl.pallas_call(
        functools.partial(finish, 2 * kr if in_turn(kr) else 0),
        out_shape=jax.ShapeDtypeStruct((2, rows, cols), jnp.float32),
        in_specs=[vmem] * 6,
        out_specs=pl.BlockSpec(memory_space=pltpu.HBM),
        scratch_shapes=[pltpu.VMEM((2, rows, LANES), jnp.float32), pltpu.SemaphoreType.DMA((3,))],
        compiler_params=pltpu.CompilerParams(vmem_limit_bytes=16 * 1024 * 1024),
    )(*held)


def solution(mesh):
    placed = (P(None, ("freq", "row"), "col"), P(None, "row", ("freq", "col")))
    return jax.shard_map(
        functools.partial(body, mesh.shape["row"], mesh.shape["col"]),
        mesh=mesh, in_specs=placed, out_specs=P(None, ("freq", "row"), "col"), check_vma=False,
    )
```

```python
import functools

import jax
import jax.numpy as jnp
from jax import lax
from jax.experimental import pallas as pl
from jax.experimental.pallas import tpu as pltpu
from jax.sharding import PartitionSpec as P

MESH = pl.DeviceIdType.MESH
LANES = 128


def split(value):
    high = value.astype(jnp.bfloat16)
    return high, (value - high.astype(jnp.float32)).astype(jnp.bfloat16)


def dot(a, b):
    return jnp.dot(a, b, preferred_element_type=jnp.float32)


def three_dots(left_hi, left_lo, w_hi, w_lo):
    return dot(left_hi, w_hi) + (dot(left_hi, w_lo) + dot(left_lo, w_hi))


def in_turn(kr):
    return kr % LANES == 0


def finish(first, done_ref, own_part, left_hi, left_lo, w_hi, w_lo, out_hbm, tail, sem):
    rows, ready = done_ref.shape[1:]
    early = pltpu.make_async_copy(done_ref, out_hbm.at[:, :, pl.ds(0, ready)], sem.at[0])
    early.start()
    copies = [early]
    half = rows // 2
    j = w_hi.shape[0] - 1
    for i in range(2):
        span = pl.ds(i * half, half)
        total = own_part[span, :] + three_dots(
            left_hi[span, first:], left_lo[span, first:], w_hi[j, first:, :], w_lo[j, first:, :])
        tail[0, span, :] = total[:, :LANES]
        tail[1, span, :] = total[:, LANES:]
        copy = pltpu.make_async_copy(
            tail.at[:, span, :], out_hbm.at[:, span, pl.ds(ready, LANES)], sem.at[1 + i])
        copy.start()
        copies.append(copy)
    for copy in copies:
        copy.wait()


def kernel(
    n_row, n_col, left_hbm, right_hbm, out_ref, own_part, left_hi, left_lo, w_hi, w_lo,
    left_f32, right_f32, own_sem, left_send, left_recv, right_send, right_recv,
):
    _, kb, rows = left_hbm.shape
    _, kr, cols = right_hbm.shape
    depth = kb * n_col
    chunks = cols // LANES
    line = n_col // 2

    x = lax.axis_index("row")
    place = lax.axis_index("col")
    z, core = place // 2, lax.rem(place, 2)
    has_next, has_prev = z + 1 < line, z >= 1

    def at(zz, cc):
        return {"col": zz * 2 + cc}

    def peer(d):
        return lax.rem(x + d, n_row)

    barrier = pltpu.get_barrier_semaphore()
    for d in range(1, n_row):
        pl.semaphore_signal(barrier, inc=1, device_id={"row": peer(d)}, device_id_type=MESH)

    @pl.when(has_next)
    def _():
        pl.semaphore_signal(barrier, inc=1, device_id=at(z + 1, core), device_id_type=MESH)

    @pl.when(has_prev)
    def _():
        pl.semaphore_signal(barrier, inc=1, device_id=at(z - 1, core), device_id_type=MESH)

    pl.semaphore_signal(barrier, inc=1, device_id=at(z, 1 - core), device_id_type=MESH)

    own_right = pltpu.make_async_copy(
        right_hbm, right_f32.at[:, pl.ds(pl.multiple_of(x * kr, 8), kr), :], own_sem.at[0])
    own_right.start()
    own_left = pltpu.make_async_copy(
        left_hbm, left_f32.at[:, pl.ds(pl.multiple_of(place * kb, 8), kb), :], own_sem.at[1])
    own_left.start()

    pl.semaphore_wait(barrier, n_row + has_next.astype(jnp.int32) + has_prev.astype(jnp.int32))

    def right_copy(d, j):
        return pltpu.make_async_remote_copy(
            src_ref=right_hbm.at[:, :, pl.ds(j * LANES, LANES)],
            dst_ref=right_f32.at[:, pl.ds(pl.multiple_of(x * kr, 8), kr), pl.ds(j * LANES, LANES)],
            send_sem=right_send.at[d - 1, j],
            recv_sem=right_recv.at[d - 1, j],
            device_id={"row": peer(d)},
            device_id_type=MESH,
        )

    def left_slot(zz, cc, part):
        return left_f32.at[part, pl.ds(pl.multiple_of((zz * 2 + cc) * kb, 8), kb), :]

    def left_copy(way, zz, cc, part, target, own=False):
        return pltpu.make_async_remote_copy(
            src_ref=left_hbm.at[part] if own else left_slot(zz, cc, part),
            dst_ref=left_slot(zz, cc, part),
            send_sem=left_send.at[way, zz, part],
            recv_sem=left_recv.at[cc, zz, part],
            device_id=target,
            device_id_type=MESH,
        )

    def up(zz, part, own=False):
        return left_copy(0, zz, core, part, at(z + 1, core), own)

    def down(zz, part, own=False):
        return left_copy(1, zz, core, part, at(z - 1, core), own)

    def across(zz, part, own=False):
        return left_copy(2, zz, core, part, at(z, 1 - core), own)

    def arrived(zz, cc, part):
        left_copy(2, zz, cc, part, at(z, 1 - core)).wait_recv()

    for part in range(2):
        @pl.when(has_next)
        def _():
            up(z, part, True).start()

        @pl.when(has_prev)
        def _():
            down(z, part, True).start()

    for j in range(chunks):
        for d in range(1, n_row):
            right_copy(d, j).start()
    for part in range(2):
        across(z, part, True).start()

    def to_weights(d, j):
        owner = peer(d)
        span = pl.ds(pl.multiple_of(owner * kr, 8), kr)
        re = split(right_f32[0, span, j * LANES:(j + 1) * LANES])
        im = split(right_f32[1, span, j * LANES:(j + 1) * LANES])
        if in_turn(kr):
            above, below = pl.ds(2 * d * kr, kr), pl.ds((2 * d + 1) * kr, kr)
        else:
            above, below = span, pl.ds(pl.multiple_of(depth + owner * kr, 8), kr)
        for w, a, b in ((w_hi, re[0], im[0]), (w_lo, re[1], im[1])):
            w[j, above, :LANES] = a
            w[j, above, LANES:] = b
            w[j, below, :LANES] = -b
            w[j, below, LANES:] = a

    def convert(g):
        for part in range(2):
            block = left_f32[part, pl.ds(pl.multiple_of(g * LANES, LANES), LANES), :].T
            high, low = split(block)
            if in_turn(kr):
                owner = g * LANES // kr
                turn = lax.rem(owner - x + n_row, n_row)
                first = (2 * turn + part) * kr + g * LANES - owner * kr
            else:
                first = part * depth + g * LANES
            where = pl.ds(pl.multiple_of(first, LANES), LANES)
            left_hi[:, where] = high
            left_lo[:, where] = low

    def early_part():
        if in_turn(kr):
            n = 2 * kr
            own_part[...] = three_dots(
                left_hi[:, :n], left_lo[:, :n], w_hi[chunks - 1, :n, :], w_lo[chunks - 1, :n, :])
        else:
            own_part[...] = jnp.zeros_like(own_part)

    def partner_arrived(zz):
        for part in range(2):
            arrived(zz, 1 - core, part)

    def settle(zz):
        partner_arrived(zz)
        if 2 * kb == LANES:
            convert(zz)

    def right_arrived(j):
        for d in range(1, n_row):
            right_copy(d, j).wait_recv()
            to_weights(n_row - d, j)

    own_right.wait()
    for j in range(chunks):
        to_weights(0, j)
    own_left.wait()

    for d in range(1, line):
        for part in range(2):
            @pl.when(z - d >= 0)
            def _():
                arrived(z - d, core, part)

                @pl.when(has_next)
                def _():
                    up(z - d, part).start()

                across(z - d, part).start()

            @pl.when(z + d < line)
            def _():
                arrived(z + d, core, part)

                @pl.when(has_prev)
                def _():
                    down(z + d, part).start()

                across(z + d, part).start()

        if d == 1:
            settle(z)
        else:
            @pl.when(z - (d - 1) >= 0)
            def _():
                settle(z - (d - 1))

            @pl.when(z + (d - 1) < line)
            def _():
                settle(z + (d - 1))

        if d - 1 < chunks - 1:
            right_arrived(d - 1)

    if line == 1:
        settle(z)
    else:
        @pl.when(z - (line - 1) >= 0)
        def _():
            settle(z - (line - 1))

        @pl.when(z + (line - 1) < line)
        def _():
            settle(z + (line - 1))

    if 2 * kb != LANES:
        for g in range(depth // LANES):
            convert(g)

    for j in range(chunks - 1):
        if j >= line - 1:
            right_arrived(j)
        total = three_dots(left_hi[...], left_lo[...], w_hi[j], w_lo[j])
        out_ref[0, :, j * LANES:(j + 1) * LANES] = total[:, :LANES]
        out_ref[1, :, j * LANES:(j + 1) * LANES] = total[:, LANES:]
        if j == chunks - 3 or (j == 0 and chunks < 3):
            early_part()
    right_arrived(chunks - 1)

    for j in range(chunks):
        for d in range(1, n_row):
            right_copy(d, j).wait_send()
    for part in range(2):
        for d in range(line):
            own = d == 0

            @pl.when(z - d >= 0)
            def _():
                @pl.when(has_next)
                def _():
                    up(z - d, part, own).wait_send()

                across(z - d, part, own).wait_send()

            @pl.when(z + d < line)
            def _():
                @pl.when(has_prev)
                def _():
                    down(z + d, part, own).wait_send()

                if d > 0:
                    across(z + d, part).wait_send()


def body(n_row, n_col, left_data, right_data):
    left = jnp.swapaxes(left_data, 1, 2)
    _, kb, rows = left.shape
    _, kr, cols = right_data.shape
    depth, chunks, line = kb * n_col, cols // LANES, n_col // 2
    vmem = pl.BlockSpec(memory_space=pltpu.VMEM)
    held = pl.pallas_call(
        functools.partial(kernel, n_row, n_col),
        out_shape=[
            jax.ShapeDtypeStruct((2, rows, cols - LANES), jnp.float32),
            jax.ShapeDtypeStruct((rows, 2 * LANES), jnp.float32),
            jax.ShapeDtypeStruct((rows, 2 * depth), jnp.bfloat16),
            jax.ShapeDtypeStruct((rows, 2 * depth), jnp.bfloat16),
            jax.ShapeDtypeStruct((chunks, 2 * depth, 2 * LANES), jnp.bfloat16),
            jax.ShapeDtypeStruct((chunks, 2 * depth, 2 * LANES), jnp.bfloat16),
        ],
        in_specs=[pl.BlockSpec(memory_space=pltpu.HBM)] * 2,
        out_specs=[vmem] * 6,
        scratch_shapes=[
            pltpu.VMEM((2, depth, rows), jnp.float32),
            pltpu.VMEM((2, depth, cols), jnp.float32),
            pltpu.SemaphoreType.DMA((2,)),
            pltpu.SemaphoreType.DMA((3, line, 2)),
            pltpu.SemaphoreType.DMA((2, line, 2)),
            pltpu.SemaphoreType.DMA((n_row - 1, chunks)),
            pltpu.SemaphoreType.DMA((n_row - 1, chunks)),
        ],
        compiler_params=pltpu.CompilerParams(
            collective_id=0, has_side_effects=True, vmem_limit_bytes=32 * 1024 * 1024),
    )(pltpu.with_memory_space_constraint(left, pltpu.HBM), pltpu.with_memory_space_constraint(right_data, pltpu.HBM))
    return pl.pallas_call(
        functools.partial(finish, 2 * kr if in_turn(kr) else 0),
        out_shape=jax.ShapeDtypeStruct((2, rows, cols), jnp.float32),
        in_specs=[vmem] * 6,
        out_specs=pl.BlockSpec(memory_space=pltpu.HBM),
        scratch_shapes=[pltpu.VMEM((2, rows, LANES), jnp.float32), pltpu.SemaphoreType.DMA((3,))],
        compiler_params=pltpu.CompilerParams(vmem_limit_bytes=16 * 1024 * 1024),
    )(*held)


def solution(mesh):
    placed = (P(None, ("freq", "row"), "col"), P(None, "row", ("freq", "col")))
    return jax.shard_map(
        functools.partial(body, mesh.shape["row"], mesh.shape["col"]),
        mesh=mesh, in_specs=placed, out_specs=P(None, ("freq", "row"), "col"), check_vma=False,
    )
```

```python
import functools

import jax
import jax.numpy as jnp
from jax import lax
from jax.experimental import pallas as pl
from jax.experimental.pallas import tpu as pltpu
from jax.sharding import PartitionSpec as P

MESH = pl.DeviceIdType.MESH
LANES = 128


def split(value):
    high = value.astype(jnp.bfloat16)
    return high, (value - high.astype(jnp.float32)).astype(jnp.bfloat16)


def dot(a, b):
    return jnp.dot(a, b, preferred_element_type=jnp.float32)


def three_dots(left_hi, left_lo, w_hi, w_lo):
    return dot(left_hi, w_hi) + (dot(left_hi, w_lo) + dot(left_lo, w_hi))


def in_turn(kr):
    return kr % LANES == 0


def staged(n_row, kr, kb, line, chunks):
    return n_row == 2 and in_turn(kr) and 2 * kb == LANES and line % 2 == 0 and chunks <= line


def finish(first, done_ref, own_part, left_hi, left_lo, w_hi, w_lo, out_hbm, tail, sem):
    rows, ready = done_ref.shape[1:]
    early = pltpu.make_async_copy(done_ref, out_hbm.at[:, :, pl.ds(0, ready)], sem.at[0])
    early.start()
    copies = [early]
    half = rows // 2
    j = w_hi.shape[0] - 1
    for i in range(2):
        span = pl.ds(i * half, half)
        total = own_part[span, :] + three_dots(
            left_hi[span, first:], left_lo[span, first:], w_hi[j, first:, :], w_lo[j, first:, :])
        tail[0, span, :] = total[:, :LANES]
        tail[1, span, :] = total[:, LANES:]
        copy = pltpu.make_async_copy(
            tail.at[:, span, :], out_hbm.at[:, span, pl.ds(ready, LANES)], sem.at[1 + i])
        copy.start()
        copies.append(copy)
    for copy in copies:
        copy.wait()


def kernel(
    n_row, n_col, left_hbm, right_hbm, out_ref, own_part, left_hi, left_lo, w_hi, w_lo,
    left_f32, right_f32, own_sem, left_send, left_recv, right_send, right_recv,
):
    _, kb, rows = left_hbm.shape
    _, kr, cols = right_hbm.shape
    depth = kb * n_col
    chunks = cols // LANES
    line = n_col // 2

    x = lax.axis_index("row")
    place = lax.axis_index("col")
    z, core = place // 2, lax.rem(place, 2)
    has_next, has_prev = z + 1 < line, z >= 1

    def at(zz, cc):
        return {"col": zz * 2 + cc}

    def peer(d):
        return lax.rem(x + d, n_row)

    barrier = pltpu.get_barrier_semaphore()
    for d in range(1, n_row):
        pl.semaphore_signal(barrier, inc=1, device_id={"row": peer(d)}, device_id_type=MESH)

    @pl.when(has_next)
    def _():
        pl.semaphore_signal(barrier, inc=1, device_id=at(z + 1, core), device_id_type=MESH)

    @pl.when(has_prev)
    def _():
        pl.semaphore_signal(barrier, inc=1, device_id=at(z - 1, core), device_id_type=MESH)

    pl.semaphore_signal(barrier, inc=1, device_id=at(z, 1 - core), device_id_type=MESH)

    own_right = pltpu.make_async_copy(
        right_hbm, right_f32.at[:, pl.ds(pl.multiple_of(x * kr, 8), kr), :], own_sem.at[0])
    own_right.start()
    own_left = pltpu.make_async_copy(
        left_hbm, left_f32.at[:, pl.ds(pl.multiple_of(place * kb, 8), kb), :], own_sem.at[1])
    own_left.start()

    pl.semaphore_wait(barrier, n_row + has_next.astype(jnp.int32) + has_prev.astype(jnp.int32))

    def right_copy(d, j):
        return pltpu.make_async_remote_copy(
            src_ref=right_hbm.at[:, :, pl.ds(j * LANES, LANES)],
            dst_ref=right_f32.at[:, pl.ds(pl.multiple_of(x * kr, 8), kr), pl.ds(j * LANES, LANES)],
            send_sem=right_send.at[d - 1, j],
            recv_sem=right_recv.at[d - 1, j],
            device_id={"row": peer(d)},
            device_id_type=MESH,
        )

    def left_slot(zz, cc, part):
        return left_f32.at[part, pl.ds(pl.multiple_of((zz * 2 + cc) * kb, 8), kb), :]

    def left_copy(way, zz, cc, part, target, own=False):
        return pltpu.make_async_remote_copy(
            src_ref=left_hbm.at[part] if own else left_slot(zz, cc, part),
            dst_ref=left_slot(zz, cc, part),
            send_sem=left_send.at[way, zz, part],
            recv_sem=left_recv.at[cc, zz, part],
            device_id=target,
            device_id_type=MESH,
        )

    def up(zz, part, own=False):
        return left_copy(0, zz, core, part, at(z + 1, core), own)

    def down(zz, part, own=False):
        return left_copy(1, zz, core, part, at(z - 1, core), own)

    def across(zz, part, own=False):
        return left_copy(2, zz, core, part, at(z, 1 - core), own)

    def arrived(zz, cc, part):
        left_copy(2, zz, cc, part, at(z, 1 - core)).wait_recv()

    for part in range(2):
        @pl.when(has_next)
        def _():
            up(z, part, True).start()

        @pl.when(has_prev)
        def _():
            down(z, part, True).start()

    for j in range(chunks):
        for d in range(1, n_row):
            right_copy(d, j).start()
    for part in range(2):
        across(z, part, True).start()

    def to_weights(d, j):
        owner = peer(d)
        span = pl.ds(pl.multiple_of(owner * kr, 8), kr)
        re = split(right_f32[0, span, j * LANES:(j + 1) * LANES])
        im = split(right_f32[1, span, j * LANES:(j + 1) * LANES])
        if in_turn(kr):
            above, below = pl.ds(2 * d * kr, kr), pl.ds((2 * d + 1) * kr, kr)
        else:
            above, below = span, pl.ds(pl.multiple_of(depth + owner * kr, 8), kr)
        for w, a, b in ((w_hi, re[0], im[0]), (w_lo, re[1], im[1])):
            w[j, above, :LANES] = a
            w[j, above, LANES:] = b
            w[j, below, :LANES] = -b
            w[j, below, LANES:] = a

    def convert(g):
        for part in range(2):
            block = left_f32[part, pl.ds(pl.multiple_of(g * LANES, LANES), LANES), :].T
            high, low = split(block)
            if in_turn(kr):
                owner = g * LANES // kr
                turn = lax.rem(owner - x + n_row, n_row)
                first = (2 * turn + part) * kr + g * LANES - owner * kr
            else:
                first = part * depth + g * LANES
            where = pl.ds(pl.multiple_of(first, LANES), LANES)
            left_hi[:, where] = high
            left_lo[:, where] = low

    early = staged(n_row, kr, kb, line, chunks)
    near_own = z // max(line // 2, 1) == x

    def piece(j, turn, fresh):
        span = slice(turn * 2 * kr, (turn + 1) * 2 * kr)
        total = three_dots(left_hi[:, span], left_lo[:, span], w_hi[j, span, :], w_lo[j, span, :])
        if j == chunks - 1:
            own_part[...] = total
            return
        where = slice(j * LANES, (j + 1) * LANES)
        for part in range(2):
            term = total[:, part * LANES:(part + 1) * LANES]
            out_ref[part, :, where] = term if fresh else out_ref[part, :, where] + term

    def partner_arrived(zz):
        for part in range(2):
            arrived(zz, 1 - core, part)

    def settle(zz):
        partner_arrived(zz)
        if 2 * kb == LANES:
            convert(zz)

    def right_arrived(j):
        for d in range(1, n_row):
            right_copy(d, j).wait_recv()
            to_weights(n_row - d, j)

    own_right.wait()
    for j in range(chunks):
        to_weights(0, j)
    own_left.wait()

    for d in range(1, line):
        for part in range(2):
            @pl.when(z - d >= 0)
            def _():
                arrived(z - d, core, part)

                @pl.when(has_next)
                def _():
                    up(z - d, part).start()

                across(z - d, part).start()

            @pl.when(z + d < line)
            def _():
                arrived(z + d, core, part)

                @pl.when(has_prev)
                def _():
                    down(z + d, part).start()

                across(z + d, part).start()

        if d == 1:
            settle(z)
        else:
            @pl.when(z - (d - 1) >= 0)
            def _():
                settle(z - (d - 1))

            @pl.when(z + (d - 1) < line)
            def _():
                settle(z + (d - 1))

        if d - 1 < chunks - 1:
            right_arrived(d - 1)

        if early and d >= line // 2:
            first = d == line // 2

            @pl.when(near_own)
            def _():
                for j in range(chunks) if first else ():
                    piece(j, 0, True)

            @pl.when(jnp.logical_not(near_own))
            def _():
                for j in range(0 if first else d - 1, min(d, chunks - 1)):
                    piece(j, 1, True)

    if line == 1:
        settle(z)
    else:
        @pl.when(z - (line - 1) >= 0)
        def _():
            settle(z - (line - 1))

        @pl.when(z + (line - 1) < line)
        def _():
            settle(z + (line - 1))

    if 2 * kb != LANES:
        for g in range(depth // LANES):
            convert(g)

    if early:
        @pl.when(near_own)
        def _():
            for j in range(chunks - 1):
                piece(j, 1, False)

        @pl.when(jnp.logical_not(near_own))
        def _():
            for j in range(chunks):
                piece(j, 0, False)
    else:
        for j in range(chunks - 1):
            if j >= line - 1:
                right_arrived(j)
            total = three_dots(left_hi[...], left_lo[...], w_hi[j], w_lo[j])
            out_ref[0, :, j * LANES:(j + 1) * LANES] = total[:, :LANES]
            out_ref[1, :, j * LANES:(j + 1) * LANES] = total[:, LANES:]
        own_part[...] = jnp.zeros_like(own_part)
    right_arrived(chunks - 1)

    for j in range(chunks):
        for d in range(1, n_row):
            right_copy(d, j).wait_send()
    for part in range(2):
        for d in range(line):
            own = d == 0

            @pl.when(z - d >= 0)
            def _():
                @pl.when(has_next)
                def _():
                    up(z - d, part, own).wait_send()

                across(z - d, part, own).wait_send()

            @pl.when(z + d < line)
            def _():
                @pl.when(has_prev)
                def _():
                    down(z + d, part, own).wait_send()

                if d > 0:
                    across(z + d, part).wait_send()


def body(n_row, n_col, left_data, right_data):
    left = jnp.swapaxes(left_data, 1, 2)
    _, kb, rows = left.shape
    _, kr, cols = right_data.shape
    depth, chunks, line = kb * n_col, cols // LANES, n_col // 2
    vmem = pl.BlockSpec(memory_space=pltpu.VMEM)
    held = pl.pallas_call(
        functools.partial(kernel, n_row, n_col),
        out_shape=[
            jax.ShapeDtypeStruct((2, rows, cols - LANES), jnp.float32),
            jax.ShapeDtypeStruct((rows, 2 * LANES), jnp.float32),
            jax.ShapeDtypeStruct((rows, 2 * depth), jnp.bfloat16),
            jax.ShapeDtypeStruct((rows, 2 * depth), jnp.bfloat16),
            jax.ShapeDtypeStruct((chunks, 2 * depth, 2 * LANES), jnp.bfloat16),
            jax.ShapeDtypeStruct((chunks, 2 * depth, 2 * LANES), jnp.bfloat16),
        ],
        in_specs=[pl.BlockSpec(memory_space=pltpu.HBM)] * 2,
        out_specs=[vmem] * 6,
        scratch_shapes=[
            pltpu.VMEM((2, depth, rows), jnp.float32),
            pltpu.VMEM((2, depth, cols), jnp.float32),
            pltpu.SemaphoreType.DMA((2,)),
            pltpu.SemaphoreType.DMA((3, line, 2)),
            pltpu.SemaphoreType.DMA((2, line, 2)),
            pltpu.SemaphoreType.DMA((n_row - 1, chunks)),
            pltpu.SemaphoreType.DMA((n_row - 1, chunks)),
        ],
        compiler_params=pltpu.CompilerParams(
            collective_id=0, has_side_effects=True, vmem_limit_bytes=32 * 1024 * 1024),
    )(pltpu.with_memory_space_constraint(left, pltpu.HBM), pltpu.with_memory_space_constraint(right_data, pltpu.HBM))
    return pl.pallas_call(
        functools.partial(finish, 2 * kr if staged(n_row, kr, kb, line, chunks) else 0),
        out_shape=jax.ShapeDtypeStruct((2, rows, cols), jnp.float32),
        in_specs=[vmem] * 6,
        out_specs=pl.BlockSpec(memory_space=pltpu.HBM),
        scratch_shapes=[pltpu.VMEM((2, rows, LANES), jnp.float32), pltpu.SemaphoreType.DMA((3,))],
        compiler_params=pltpu.CompilerParams(vmem_limit_bytes=16 * 1024 * 1024),
    )(*held)


def solution(mesh):
    placed = (P(None, ("freq", "row"), "col"), P(None, "row", ("freq", "col")))
    return jax.shard_map(
        functools.partial(body, mesh.shape["row"], mesh.shape["col"]),
        mesh=mesh, in_specs=placed, out_specs=P(None, ("freq", "row"), "col"), check_vma=False,
    )
```
